256 devices in a mesh: brick: 32 (over z, y_hi, core), chan: 8 (over y_lo, x).
Axes of the slice: x: 4, y: 4 (y_hi: 2, y_lo: 2; y = y_hi * 2 + y_lo), z: 8, core: 2. Of those that a mesh axis runs over, the one named last changes fastest.
Arguments:
- volume: bfloat16 [64, 64, 64, 256], P('brick', 'chan'), may hold values from -6 to 6
- first_weight: bfloat16 [3, 3, 3, 256, 256], replicated, may hold values from -0.078125 to 0.078125
- second_weight: bfloat16 [3, 3, 3, 256, 256], replicated, may hold values from -0.078125 to 0.078125
- coarse_weight: bfloat16 [3, 3, 3, 256, 512], P(None, None, None, None, 'chan'), may hold values from -0.078125 to 0.078125
- projection: bfloat16 [512, 256], P('chan'), may hold values from -0.25 to 0.25
Outputs:
- merged: bfloat16 [64, 64, 64, 256], P('brick', 'chan')
The draws below stay inside these ranges and needn't reach their ends.
All inputs are finite; a program needn't handle non-finite values.
Results may differ from the reference program's by a relative error of at most 0.011.
Values may be sent and summed in bfloat16 or wider, within the bound.
A program may use at most 64 MiB of HBM per device.

```python
import jax
import jax.numpy as jnp
from jax import lax

C = 256
CO = 512
NZ = 64
NX = 64
NY = 64


def steps_of(stream_key, shape, split, least, high):
    gain = 1.0
    for dim, parts in split:
        draws = jax.random.uniform(jax.random.fold_in(jax.random.fold_in(stream_key, 6), dim), (parts,), jnp.float32, least / len(split), high / len(split))
        gain = gain * jnp.repeat(jnp.exp(draws), shape[dim] // parts).reshape((-1,) + (1,) * (len(shape) - 1 - dim))
    return gain


def noise(own_key, extent, deviation, bound, split=(), dtype=jnp.bfloat16):
    values = jax.random.normal(own_key, extent, jnp.float32) * deviation
    if len(split) > 0:
        values = steps_of(own_key, extent, split, -0.22, 0.18) * values
    return jnp.clip(values, min=-bound, max=bound).astype(dtype)


def setup_inputs(seed: int = 0) -> dict:
    key_of = jax.random.split(jax.random.key(seed), 6)
    volume = noise(key_of[0], (NX, NY, NZ, C), 1.0, 6.0, ((0, 32), (1, 8)))
    first_weight = noise(key_of[1], (3, 3, 3, C, C), (27 * C) ** -0.5, 0.078125)
    second_weight = noise(key_of[2], (3, 3, 3, C, C), (27 * C) ** -0.5, 0.078125)
    coarse_weight = noise(key_of[3], (3, 3, 3, C, CO), (27 * C) ** -0.5, 0.078125, ((4, 8),))
    projection = noise(key_of[4], (CO, C), CO ** -0.5, 0.25, ((0, 8),))
    return {"volume": volume, "first_weight": first_weight, "second_weight": second_weight, "coarse_weight": coarse_weight, "projection": projection}


def convolve(field, weight):
    source = field.astype(jnp.float32)[None]
    kernel = weight.astype(jnp.float32)
    result = lax.conv_general_dilated(source, kernel, (1, 1, 1), "SAME", dimension_numbers=("NDHWC", "DHWIO", "NDHWC"), precision=lax.Precision.HIGHEST)
    return result[0]


def reference(volume, first_weight, second_weight, coarse_weight, projection):
    layer_one = jnp.maximum(convolve(volume, first_weight), 0.0).astype(jnp.bfloat16)
    skipped = jnp.maximum(convolve(layer_one, second_weight), 0.0).astype(jnp.bfloat16)
    size_x, size_y, size_z, channels_in = skipped.shape
    blocks = skipped.astype(jnp.float32).reshape(size_x // 2, 2, size_y // 2, 2, size_z // 2, 2, channels_in)
    pooled = jnp.mean(blocks, axis=(1, 3, 5)).astype(jnp.bfloat16)
    coarse = jnp.maximum(convolve(pooled, coarse_weight), 0.0).astype(jnp.bfloat16)
    flat = coarse.reshape(-1, coarse.shape[3])
    lifted = jnp.dot(flat, projection, preferred_element_type=jnp.float32).reshape(size_x // 2, size_y // 2, size_z // 2, channels_in)
    upsampled = jnp.repeat(jnp.repeat(jnp.repeat(lifted, 2, axis=0), 2, axis=1), 2, axis=2)
    return (skipped.astype(jnp.float32) + upsampled).astype(jnp.bfloat16)
```

```python
import functools

import jax
import jax.numpy as jnp
from jax import lax
from jax.experimental import pallas as pl
from jax.experimental.pallas import tpu as pltpu
from jax.sharding import PartitionSpec as P

MESH = pl.DeviceIdType.MESH
F32 = jnp.float32
BF16 = jnp.bfloat16


def level(
    nb, nc, vol, w1h, w2h, wch, prh, out,
    x, y, w1, w2, wc, wcr, pg, xc, con, rec, prj, prr, acc1, acc2, skip, tmp,
    loc, s1, r1, s2, r2, sp, rp, sg, rg, sc, rc,
):
    b = lax.axis_index("brick")
    c = lax.axis_index("chan")
    q = lax.rem(b, 2)
    slow = lax.rem(b + 2 * q - 1 + nb, nb)
    fast = lax.rem(b + 1 - 2 * q + nb, nb)
    below = lax.rem(b - 1 + nb, nb)
    above = lax.rem(b + 1, nb)

    def chan(d):
        return lax.rem(c + d, nc)

    loads = [
        pltpu.make_async_copy(vol.at[q], x.at[1, 1, pl.ds(1, 8)], loc.at[0]),
        pltpu.make_async_copy(vol.at[1 - q], x.at[1, 2, pl.ds(1, 8)], loc.at[1]),
        pltpu.make_async_copy(w1h, w1, loc.at[2]),
        pltpu.make_async_copy(prh, prj.at[c], loc.at[3]),
        pltpu.make_async_copy(wch, wc, loc.at[4]),
        pltpu.make_async_copy(w2h, w2, loc.at[5]),
    ]
    for load in loads:
        load.start()

    barrier = pltpu.get_barrier_semaphore()
    for brick in (b, below, above):
        for d in range(nc):
            if brick is b and d == 0:
                continue
            pl.semaphore_signal(barrier, inc=1, device_id=(brick, chan(d)), device_id_type=MESH)
    loads[0].wait()
    loads[1].wait()
    pl.semaphore_wait(barrier, 3 * nc - 1)

    right, left = chan(1), chan(nc - 1)

    def halo(buf, ss, rs, u):
        far, dest = (slow, 0) if u == 0 else (fast, 3)
        p = u + 1
        plans = [
            (p, 8, 1, p, 0, (b, right)),
            (p, 1, 1, p, 9, (b, left)),
            (p, 8, 1, dest, 0, (far, right)),
            (p, 1, 1, dest, 9, (far, left)),
            (p, 1, 8, dest, 1, (far, c)),
        ]
        return [
            pltpu.make_async_remote_copy(
                buf.at[1, src, pl.ds(row, n)], buf.at[1, dst, pl.ds(to, n)],
                ss.at[u, i], rs.at[u, i], device_id=who, device_id_type=MESH,
            )
            for i, (src, row, n, dst, to, who) in enumerate(plans)
        ]

    first = [halo(x, s1, r1, 0), halo(x, s1, r1, 1)]
    for copies in first:
        for copy in copies:
            copy.start()

    loads[3].wait()
    gifts = [
        pltpu.make_async_remote_copy(
            prj.at[c], prj.at[c], sp.at[d], rp.at[d], device_id=(b, chan(d)), device_id_type=MESH
        )
        for d in range(1, nc)
    ]
    for gift in gifts:
        gift.start()

    zero_row = jnp.zeros((1, 256), BF16)

    def spread(buf, p, row, v):
        buf[0, p, row] = jnp.concatenate([zero_row, v[:-1]], axis=0)
        buf[2, p, row] = jnp.concatenate([v[1:], zero_row], axis=0)

    def spread_rows(buf, p, start, n):
        def body(i, _):
            spread(buf, p, start + i, buf[1, p, start + i])
            return 0
        lax.fori_loop(0, n, body, 0)

    has_low, has_high = c > 0, c < nc - 1
    has_slow = jnp.logical_and(slow != b + nb - 1, slow != b + 1 - nb)

    def masked(buf, p, row, valid):
        v = jnp.where(valid, buf[1, p, row].astype(F32), 0.0).astype(BF16)
        buf[1, p, row] = v
        spread(buf, p, row, v)

    def edge_rows(buf, copies, u):
        copies[u][0].wait_recv()
        copies[u][1].wait_recv()
        masked(buf, u + 1, 0, has_low)
        masked(buf, u + 1, 9, has_high)

    def plane_halo(buf, copies, u):
        p = 0 if u == 0 else 3
        for k in (2, 3, 4):
            copies[u][k].wait_recv()
        if u == 0:
            masked(buf, p, 0, jnp.logical_and(has_low, has_slow))
            masked(buf, p, 9, jnp.logical_and(has_high, has_slow))

            def body(i, _):
                masked(buf, p, 1 + i, has_slow)
                return 0
            lax.fori_loop(0, 8, body, 0)
        else:
            masked(buf, p, 0, has_low)
            masked(buf, p, 9, has_high)
            spread_rows(buf, p, 1, 8)

    def taps(buf, w, u, i):
        lhs = jnp.concatenate(
            [buf[k, u + i, j : j + 8].reshape(512, 256) for j in range(3) for k in range(3)], axis=1
        )
        return jnp.dot(lhs, w[i + q * (2 - 2 * i)], preferred_element_type=F32)

    def finish_one(u):
        def body(r, _):
            v = jnp.maximum(acc1[u, pl.ds(pl.multiple_of(r * 64, 64), 64)], 0.0).astype(BF16)
            y[1, u + 1, 1 + r] = v
            spread(y, u + 1, 1 + r, v)
            return 0
        lax.fori_loop(0, 8, body, 0)

    spread_rows(x, 1, 1, 8)
    spread_rows(x, 2, 1, 8)
    loads[2].wait()
    edge_rows(x, first, 1)
    edge_rows(x, first, 0)
    acc1[1] = taps(x, w1, 1, 0) + taps(x, w1, 1, 1)
    acc1[0] = taps(x, w1, 0, 1) + taps(x, w1, 0, 2)
    plane_halo(x, first, 1)
    acc1[1] += taps(x, w1, 1, 2)
    finish_one(1)
    second = [halo(y, s2, r2, 0), halo(y, s2, r2, 1)]
    for copy in second[1]:
        copy.start()
    plane_halo(x, first, 0)
    acc1[0] += taps(x, w1, 0, 0)
    finish_one(0)
    for copy in second[0]:
        copy.start()

    loads[5].wait()
    edge_rows(y, second, 1)
    acc2[1] = taps(y, w2, 1, 1)
    acc2[0] = taps(y, w2, 0, 2)
    plane_halo(y, second, 1)
    acc2[1] += taps(y, w2, 1, 2)
    edge_rows(y, second, 0)
    acc2[1] += taps(y, w2, 1, 0)
    acc2[0] += taps(y, w2, 0, 1)

    loads[4].wait()
    none = jnp.zeros((256, 64), BF16)

    def weight_block(jk, _):
        wcr[pl.ds(pl.multiple_of(jk * 256, 256), 256)] = jnp.concatenate(
            [wc[jk], wc[9 + jk], wc[18 + jk], none], axis=1
        )
        return 0
    lax.fori_loop(0, 9, weight_block, 0)
    for gift in gifts:
        gift.wait()
    prr[...] = jnp.zeros_like(prr)
    for k in range(nc):
        prr[pl.ds(k * 128, 64), 0:256] = prj[k]
        prr[pl.ds(k * 128 + 64, 64), 256:512] = prj[k]

    plane_halo(y, second, 0)
    acc2[0] += taps(y, w2, 0, 0)

    def pool(r, _):
        total = jnp.zeros((64, 256), F32)
        for u in range(2):
            for s in range(2):
                rows = pl.ds(pl.multiple_of(r * 128 + s * 64, 64), 64)
                v = jnp.maximum(acc2[u, rows], 0.0).astype(BF16)
                skip[u, 2 * r + s] = v
                total = total + v.astype(F32)
        halves = []
        for h in range(2):
            tmp[r, h] = total[:, h * 128 : h * 128 + 128]
            even = tmp[r, h, pl.ds(0, 32, stride=2)]
            odd = tmp[r, h, pl.ds(1, 32, stride=2)]
            halves.append(((even + odd) * 0.125).astype(BF16))
        pg[c, r] = jnp.concatenate(halves, axis=1)
        return 0
    lax.fori_loop(0, 4, pool, 0)

    shares = [
        pltpu.make_async_remote_copy(
            pg.at[c], pg.at[c], sg.at[d], rg.at[d], device_id=(b, chan(d)), device_id_type=MESH
        )
        for d in range(1, nc)
    ]
    for share in shares:
        share.start()

    blank = jnp.zeros((32, 256), BF16)
    for k in range(3):
        xc[k, 0] = blank
        xc[k, 4 * nc + 1] = blank

    def place(block):
        def body(r, _):
            v = pg[block, r]
            row = 1 + block * 4 + r
            xc[1, row] = v
            xc[0, row] = jnp.concatenate([zero_row, v[:-1]], axis=0)
            xc[2, row] = jnp.concatenate([v[1:], zero_row], axis=0)
            return 0
        lax.fori_loop(0, 4, body, 0)

    place(c)
    for d in range(1, nc):
        shares[d - 1].wait_recv()
        place(chan(nc - d))

    lane = lax.broadcasted_iota(jnp.int32, (64, 128), 1)
    group = 4

    def coarse(g, _):
        row = g * 4 * group
        lhs = jnp.concatenate(
            [
                xc[k, pl.ds(row + j, 4 * group)].reshape(128 * group, 256)
                for j in range(3) for k in range(3)
            ],
            axis=1,
        )
        got = jnp.dot(lhs, wcr[...], preferred_element_type=F32)
        for h in range(group):
            lo = got[h * 128 : h * 128 + 64]
            hi = got[h * 128 + 64 : h * 128 + 128]
            block = g * group + h
            con[0, block] = jnp.where(lane < 64, lo[:, :128], pltpu.roll(hi[:, :128], 64, 1)).astype(BF16)
            con[1, block] = jnp.where(lane < 64, pltpu.roll(lo[:, :128], 64, 1), hi[:, :128]).astype(BF16)
            con[2, block] = jnp.where(lane < 64, lo[:, 128:], pltpu.roll(hi[:, 128:], 64, 1)).astype(BF16)
        return 0
    lax.fori_loop(0, nc // group, coarse, 0)

    parts = []
    for i, brick in ((0, above), (1, b), (2, below)):
        for d in range(nc):
            if i == 1 and d == 0:
                continue
            copy = pltpu.make_async_remote_copy(
                con.at[i, chan(d)], rec.at[i, c], sc.at[i, d], rc.at[i, d],
                device_id=(brick, chan(d)), device_id_type=MESH,
            )
            copy.start()
            parts.append(copy)
    rec[1, c] = con[1, c]
    for part in parts:
        part.wait_recv()

    from_below, from_above = b > 0, b < nb - 1
    cols = []
    for k in range(nc):
        total = rec[1, k].astype(F32)
        total = total + jnp.where(from_below, rec[0, k].astype(F32), 0.0)
        total = total + jnp.where(from_above, rec[2, k].astype(F32), 0.0)
        cols.append(jnp.maximum(total, 0.0).astype(BF16))
    lifted = jnp.dot(jnp.concatenate(cols, axis=1), prr[...], preferred_element_type=F32)
    for r in range(4):
        for h in range(2):
            lanes = (r // 2) * 256 + h * 128
            piece = lifted[(r % 2) * 32 : (r % 2) * 32 + 32, lanes : lanes + 128]
            tmp[r, h, pl.ds(0, 32, stride=2)] = piece
            tmp[r, h, pl.ds(1, 32, stride=2)] = piece

    def merge(n, _):
        u = n // 8
        r = lax.rem(n, 8)
        plane = u + q * (1 - 2 * u)
        out[plane, r] = (
            skip[u, r].astype(F32) + jnp.concatenate([tmp[r // 2, 0], tmp[r // 2, 1]], axis=1)
        ).astype(BF16)
        return 0
    lax.fori_loop(0, 16, merge, 0)

    for copies in first + second:
        for copy in copies:
            copy.wait_send()
    for share in shares:
        share.wait_send()
    for part in parts:
        part.wait_send()


def shards(nb, nc, volume, first_weight, second_weight, coarse_weight, projection):
    dma = pltpu.SemaphoreType.DMA
    return pl.pallas_call(
        functools.partial(level, nb, nc),
        out_shape=jax.ShapeDtypeStruct(volume.shape, BF16),
        in_specs=[pl.BlockSpec(memory_space=pl.ANY)] * 5,
        out_specs=pl.BlockSpec(memory_space=pltpu.VMEM),
        scratch_shapes=[
            pltpu.VMEM((3, 4, 10, 64, 256), BF16),
            pltpu.VMEM((3, 4, 10, 64, 256), BF16),
            pltpu.VMEM((3, 2304, 256), BF16),
            pltpu.VMEM((3, 2304, 256), BF16),
            pltpu.VMEM((27, 256, 64), BF16),
            pltpu.VMEM((2304, 256), BF16),
            pltpu.VMEM((nc, 4, 32, 256), BF16),
            pltpu.VMEM((3, 4 * nc + 2, 32, 256), BF16),
            pltpu.VMEM((3, nc, 64, 128), BF16),
            pltpu.VMEM((3, nc, 64, 128), BF16),
            pltpu.VMEM((nc, 64, 256), BF16),
            pltpu.VMEM((nc * 128, 512), BF16),
            pltpu.VMEM((2, 512, 256), F32),
            pltpu.VMEM((2, 512, 256), F32),
            pltpu.VMEM((2, 8, 64, 256), BF16),
            pltpu.VMEM((4, 2, 64, 128), F32),
            dma((6,)),
            dma((2, 5)),
            dma((2, 5)),
            dma((2, 5)),
            dma((2, 5)),
            dma((nc,)),
            dma((nc,)),
            dma((nc,)),
            dma((nc,)),
            dma((3, nc)),
            dma((3, nc)),
        ],
        compiler_params=pltpu.CompilerParams(
            collective_id=0, has_side_effects=True, vmem_limit_bytes=56 << 20
        ),
        name="level",
    )(
        volume,
        first_weight.reshape(3, 2304, 256),
        second_weight.reshape(3, 2304, 256),
        coarse_weight.reshape(27, 256, 64),
        projection,
    )


def solution(mesh):
    in_specs = (
        P("brick", "chan", None, None),
        P(),
        P(),
        P(None, None, None, None, "chan"),
        P("chan", None),
    )
    out_specs = P("brick", "chan", None, None)
    body = functools.partial(shards, mesh.shape["brick"], mesh.shape["chan"])
    return jax.shard_map(body, mesh=mesh, in_specs=in_specs, out_specs=out_specs, check_vma=False)
```

```python
import functools

import jax
import jax.numpy as jnp
from jax import lax
from jax.experimental import pallas as pl
from jax.experimental.pallas import tpu as pltpu
from jax.sharding import PartitionSpec as P

MESH = pl.DeviceIdType.MESH
F32 = jnp.float32
BF16 = jnp.bfloat16


def level(
    nb, nc, vol, w1h, w2h, wch, prh, skip, lift,
    x, y, w1, w2, wc, xc, con, rec, prj, acc1, acc2, tmp,
    loc, s1, r1, s2, r2, sp, rp, sw, rw, sf, rf, sg, rg, sc, rc, near,
):
    b = lax.axis_index("brick")
    c = lax.axis_index("chan")
    q = lax.rem(b, 2)
    slow = lax.rem(b + 2 * q - 1 + nb, nb)
    fast = lax.rem(b + 1 - 2 * q + nb, nb)
    below = lax.rem(b - 1 + nb, nb)
    above = lax.rem(b + 1, nb)
    nx = nc // 2
    row_of, place = c // nx, lax.rem(c, nx)

    def chan(d):
        return lax.rem(c + d, nc)

    loads = [
        pltpu.make_async_copy(vol.at[q], x.at[1, 1, pl.ds(1, 8)], loc.at[0]),
        pltpu.make_async_copy(vol.at[1 - q], x.at[1, 2, pl.ds(1, 8)], loc.at[1]),
        pltpu.make_async_copy(w1h, w1, loc.at[2]),
        pltpu.make_async_copy(prh, prj.at[c], loc.at[3]),
        pltpu.make_async_copy(wch, wc.at[:, pl.ds(pl.multiple_of(place * 64, 64), 64)], loc.at[4]),
        pltpu.make_async_copy(w2h, w2, loc.at[5]),
    ]
    for k in (0, 1):
        loads[k].start()

    right, left, across = chan(1), chan(nc - 1), chan(nx)
    barrier = pltpu.get_barrier_semaphore()
    for who in ((slow, c), (b, right), (b, left), (b, across), (fast, right), (fast, left), (fast, c)):
        pl.semaphore_signal(barrier, inc=1, device_id=who, device_id_type=MESH)
    loads[0].wait()
    loads[1].wait()
    pl.semaphore_wait(barrier, 7)

    def halo(buf, ss, rs):
        plans = [(1, 1 + i, 1, 0, 1 + i, (slow, c)) for i in range(8)]
        plans += [
            (1, 1, 1, 1, 9, (b, left)),
            (1, 8, 1, 1, 0, (b, right)),
            (2, 1, 1, 2, 9, (b, left)),
            (2, 8, 1, 2, 0, (b, right)),
            (2, 1, 8, 3, 1, (fast, c)),
            (2, 1, 1, 3, 9, (fast, left)),
            (2, 8, 1, 3, 0, (fast, right)),
            (1, 1, 1, 0, 9, (slow, left)),
            (1, 8, 1, 0, 0, (slow, right)),
        ]
        return [
            pltpu.make_async_remote_copy(
                buf.at[1, src, pl.ds(row, n)], buf.at[1, dst, pl.ds(to, n)],
                ss.at[i], rs.at[i], device_id=who, device_id_type=MESH,
            )
            for i, (src, row, n, dst, to, who) in enumerate(plans)
        ]

    def start(copies, *which):
        for k in which:
            copies[k].start()

    def arrived(copies, *which):
        for k in which:
            copies[k].wait_recv()

    first = halo(x, s1, r1)
    start(first, 12, 8, 9, 10, 11, 0, 1, 2, 3, 4, 5, 6, 7, 13, 14)
    for who in (right, left, across):
        pl.semaphore_signal(near, inc=1, device_id=(b, who), device_id_type=MESH)
    for k in (2, 4, 3, 5):
        loads[k].start()

    gifts = [
        pltpu.make_async_remote_copy(
            prj.at[c], prj.at[c], sp.at[d], rp.at[d], device_id=(b, chan(d)), device_id_type=MESH
        )
        for d in range(1, nc)
    ]

    def shard(owner, core):
        return pl.ds(pl.multiple_of(owner * 64 + core * 32, 32), 32)

    def along(d):
        return lax.rem(place + d, nx)

    blocks = (pl.ds(0, 14), pl.ds(14, 13))

    def ring(slot, source, part, owner, to):
        return pltpu.make_async_remote_copy(
            source, wc.at[blocks[part], shard(owner, q)], sw.at[slot], rw.at[slot],
            device_id=(b, row_of * nx + to), device_id_type=MESH,
        )

    ahead, behind = along(1), along(nx - 1)
    mine = [wch.at[part, pl.ds(pl.multiple_of(q * 32, 32), 32)] for part in blocks]
    weights = [
        ring(0, mine[0], 0, place, ahead),
        ring(1, mine[1], 1, place, behind),
        ring(2, mine[1], 1, place, ahead),
        ring(3, mine[0], 0, place, behind),
        ring(4, wc.at[blocks[0], shard(behind, q)], 0, behind, ahead),
        ring(5, wc.at[blocks[1], shard(ahead, q)], 1, ahead, behind),
    ]
    passed = [
        pltpu.make_async_remote_copy(
            wc.at[:, shard(owner, q)], wc.at[:, shard(owner, q)], sf.at[d], rf.at[d],
            device_id=(fast, c), device_id_type=MESH,
        )
        for d, owner in enumerate((behind, ahead, along(nx // 2)))
    ]

    zero_row = jnp.zeros((1, 256), BF16)

    def spread(buf, p, row, v):
        buf[0, p, row] = jnp.concatenate([zero_row, v[:-1]], axis=0)
        buf[2, p, row] = jnp.concatenate([v[1:], zero_row], axis=0)

    def spread_rows(buf, p, start, n):
        def body(i, _):
            spread(buf, p, start + i, buf[1, p, start + i])
            return 0
        lax.fori_loop(0, n, body, 0)

    has_low, has_high = c > 0, c < nc - 1
    has_slow = jnp.logical_and(slow != b + nb - 1, slow != b + 1 - nb)

    def masked(buf, p, row, valid):
        v = jnp.where(valid, buf[1, p, row].astype(F32), 0.0).astype(BF16)
        buf[1, p, row] = v
        spread(buf, p, row, v)

    def edge_rows(buf, copies, u):
        arrived(copies, 8 + 2 * u, 9 + 2 * u)
        masked(buf, u + 1, 9, has_high)
        masked(buf, u + 1, 0, has_low)

    def slow_halo(buf, copies, part):
        if part == 0:
            arrived(copies, 0, 1, 2, 3, 4, 16)
            masked(buf, 0, 0, has_low)
            spread_rows(buf, 0, 1, 5)
        else:
            arrived(copies, 5, 6, 7, 15)
            masked(buf, 0, 9, has_high)
            spread_rows(buf, 0, 6, 3)

    def fast_halo(buf, copies):
        arrived(copies, 12, 13, 14)
        masked(buf, 3, 0, has_low)
        masked(buf, 3, 9, has_high)
        spread_rows(buf, 3, 1, 8)

    def taps(buf, w, u, i, row=0, n=8):
        lhs = jnp.concatenate(
            [
                buf[k, u + i, row + j : row + j + n].reshape(n * 64, 256)
                for j in range(3) for k in range(3)
            ],
            axis=1,
        )
        return jnp.dot(lhs, w[i + q * (2 - 2 * i)], preferred_element_type=F32)

    def slow_taps(buf, w, row, n):
        return jnp.where(has_slow, taps(buf, w, 0, 0, row, n), 0.0)

    def finish_one(u, start=0, n=8):
        def body(r, _):
            v = jnp.maximum(acc1[u, pl.ds(pl.multiple_of(r * 64, 64), 64)], 0.0).astype(BF16)
            y[1, u + 1, 1 + r] = v
            spread(y, u + 1, 1 + r, v)
            return 0
        lax.fori_loop(start, start + n, body, 0)

    pl.semaphore_wait(near, 3)
    start(first, 15, 16)
    start(weights, 0, 1, 2, 3)
    spread_rows(x, 1, 1, 8)
    spread_rows(x, 2, 1, 8)
    edge_rows(x, first, 0)
    edge_rows(x, first, 1)
    loads[2].wait()
    acc1[1] = taps(x, w1, 1, 0) + taps(x, w1, 1, 1)
    fast_halo(x, first)
    acc1[1] += taps(x, w1, 1, 2)
    finish_one(1)
    second = halo(y, s2, r2)
    start(second, 12, 10, 11, 13, 14)
    acc1[0] = taps(x, w1, 0, 1) + taps(x, w1, 0, 2)
    arrived(weights, 0, 1)
    start(weights, 4, 5)
    slow_halo(x, first, 0)
    acc1[0, :256] += slow_taps(x, w1, 0, 4)
    finish_one(0, 0, 4)
    start(second, 0, 15, 8, 1, 2, 3)
    slow_halo(x, first, 1)
    acc1[0, 256:] += slow_taps(x, w1, 4, 4)
    finish_one(0, 4, 4)
    start(second, 16, 9, 4, 5, 6, 7)

    loads[3].wait()
    for gift in gifts:
        gift.start()

    loads[5].wait()
    edge_rows(y, second, 1)
    acc2[1] = taps(y, w2, 1, 1)
    acc2[0] = taps(y, w2, 0, 2)
    fast_halo(y, second)
    acc2[1] += taps(y, w2, 1, 2)
    edge_rows(y, second, 0)
    acc2[1] += taps(y, w2, 1, 0)
    acc2[0] += taps(y, w2, 0, 1)
    loads[4].wait()
    arrived(weights, 2, 3)
    start(passed, 0, 1)
    slow_halo(y, second, 0)
    slow_halo(y, second, 1)
    acc2[0] += slow_taps(y, w2, 0, 8)
    def pool(r, _):
        total = jnp.zeros((64, 256), F32)
        for u in range(2):
            for s in range(2):
                rows = pl.ds(pl.multiple_of(r * 128 + s * 64, 64), 64)
                v = jnp.maximum(acc2[u, rows], 0.0).astype(BF16)
                skip[u + q * (1 - 2 * u), 2 * r + s] = v
                total = total + v.astype(F32)
        halves = []
        for h in range(2):
            tmp[r, h] = total[:, h * 128 : h * 128 + 128]
            even = tmp[r, h, pl.ds(0, 32, stride=2)]
            odd = tmp[r, h, pl.ds(1, 32, stride=2)]
            halves.append(((even + odd) * 0.125).astype(BF16))
        xc[1, row_of, 1 + r] = jnp.concatenate(halves, axis=1)
        return 0
    lax.fori_loop(0, 4, pool, 0)

    partner = across
    shares = [
        pltpu.make_async_remote_copy(
            xc.at[1, row_of, pl.ds(row, n)], xc.at[1, slot, pl.ds(to, n)],
            sg.at[i], rg.at[i], device_id=(b, who), device_id_type=MESH,
        )
        for i, (row, n, slot, to, who) in enumerate(
            [
                (1, 4, row_of, 1, partner),
                (4, 1, chan(1) // nx, 0, chan(1)),
                (4, 1, chan(1) // nx, 0, chan(1 + nx)),
                (1, 1, chan(nc - 1) // nx, 5, chan(nc - 1)),
                (1, 1, chan(nc - 1) // nx, 5, chan(nx - 1)),
            ]
        )
    ]
    for share in shares:
        share.start()
    arrived(weights, 4, 5)
    start(passed, 2)
    for share in shares:
        share.wait_recv()

    def widen(h, r, v):
        xc[0, h, r] = jnp.concatenate([zero_row, v[:-1]], axis=0)
        xc[2, h, r] = jnp.concatenate([v[1:], zero_row], axis=0)

    for h in range(2):
        block = h * nx + place
        for r, valid in ((0, block > 0), (5, block < nc - 1)):
            v = jnp.where(valid, xc[1, h, r].astype(F32), 0.0).astype(BF16)
            xc[1, h, r] = v
            widen(h, r, v)

        def coarse_row(r, _):
            widen(h, r, xc[1, h, r])
            return 0
        lax.fori_loop(1, 5, coarse_row, 0)
    arrived(passed, 0, 1, 2)

    parts = []
    for role, (tap, brick) in enumerate(((2 - 2 * q, slow), (1, b), (2 * q, fast))):
        lhs = jnp.concatenate(
            [xc[k, :, j : j + 4].reshape(256, 256) for j in range(3) for k in range(3)], axis=1
        )
        rhs = jnp.concatenate([wc[tap * 9 + jk] for jk in range(9)], axis=1)
        got = lax.dot_general(lhs, rhs, (((1,), (1,)), ((), ())), preferred_element_type=F32)
        con[role] = got.astype(BF16).reshape(2, 128, 256)
        for t, slot, who in ((0, row_of, c), (1, 1 - row_of, partner)):
            if role == 1 and t == 0:
                rec[1, row_of] = con[1, row_of]
                continue
            copy = pltpu.make_async_remote_copy(
                con.at[role, slot], rec.at[role, row_of], sc.at[role, t], rc.at[role, t],
                device_id=(brick, who), device_id_type=MESH,
            )
            copy.start()
            parts.append(copy)
    arrived(gifts, *range(nc - 1))
    for part in parts:
        part.wait_recv()

    cols = []
    for h in range(2):
        total = rec[1, h].astype(F32) + rec[2, h].astype(F32)
        total = total + jnp.where(has_slow, rec[0, h].astype(F32), 0.0)
        cols.append(jnp.maximum(total, 0.0).astype(BF16))
    lifted = jnp.dot(
        jnp.concatenate(cols, axis=1), prj[...].reshape(nc * 64, 256), preferred_element_type=F32
    )
    lift[...] = lifted.reshape(4, 32, 256)

    for copy in first + second + gifts + shares + parts + weights + passed:
        copy.wait_send()


def merge(skip, lift, out, tmp):
    for r in range(4):
        for h in range(2):
            piece = lift[r, :, h * 128 : h * 128 + 128]
            tmp[h, pl.ds(0, 32, stride=2)] = piece
            tmp[h, pl.ds(1, 32, stride=2)] = piece
        wide = jnp.concatenate([tmp[0], tmp[1]], axis=1)
        for u in range(2):
            for s in range(2):
                out[u, 2 * r + s] = (skip[u, 2 * r + s].astype(F32) + wide).astype(BF16)


def shards(nb, nc, volume, first_weight, second_weight, coarse_weight, projection):
    dma = pltpu.SemaphoreType.DMA
    skip, lift = pl.pallas_call(
        functools.partial(level, nb, nc),
        out_shape=(
            jax.ShapeDtypeStruct(volume.shape, BF16),
            jax.ShapeDtypeStruct((4, 32, 256), F32),
        ),
        in_specs=[pl.BlockSpec(memory_space=pl.ANY)] * 5,
        out_specs=(pl.BlockSpec(memory_space=pltpu.VMEM),) * 2,
        scratch_shapes=[
            pltpu.VMEM((3, 4, 10, 64, 256), BF16),
            pltpu.VMEM((3, 4, 10, 64, 256), BF16),
            pltpu.VMEM((3, 2304, 256), BF16),
            pltpu.VMEM((3, 2304, 256), BF16),
            pltpu.VMEM((27, 256, 256), BF16),
            pltpu.VMEM((3, 2, 6, 32, 256), BF16),
            pltpu.VMEM((3, 2, 128, 256), BF16),
            pltpu.VMEM((3, 2, 128, 256), BF16),
            pltpu.VMEM((nc, 64, 256), BF16),
            pltpu.VMEM((2, 512, 256), F32),
            pltpu.VMEM((2, 512, 256), F32),
            pltpu.VMEM((4, 2, 64, 128), F32),
            dma((6,)),
            dma((17,)),
            dma((17,)),
            dma((17,)),
            dma((17,)),
            dma((nc,)),
            dma((nc,)),
            dma((6,)),
            dma((6,)),
            dma((3,)),
            dma((3,)),
            dma((5,)),
            dma((5,)),
            dma((3, 2)),
            dma((3, 2)),
            pltpu.SemaphoreType.REGULAR,
        ],
        compiler_params=pltpu.CompilerParams(
            collective_id=0, has_side_effects=True, vmem_limit_bytes=56 << 20
        ),
        name="level",
    )(
        volume,
        first_weight.reshape(3, 2304, 256),
        second_weight.reshape(3, 2304, 256),
        jnp.swapaxes(coarse_weight, 3, 4).reshape(27, 64, 256),
        projection,
    )
    return pl.pallas_call(
        merge,
        out_shape=jax.ShapeDtypeStruct(volume.shape, BF16),
        scratch_shapes=[pltpu.VMEM((2, 64, 128), F32)],
        name="merge",
    )(skip, lift)


def solution(mesh):
    in_specs = (
        P("brick", "chan", None, None),
        P(),
        P(),
        P(None, None, None, None, "chan"),
        P("chan", None),
    )
    out_specs = P("brick", "chan", None, None)
    body = functools.partial(shards, mesh.shape["brick"], mesh.shape["chan"])
    return jax.shard_map(body, mesh=mesh, in_specs=in_specs, out_specs=out_specs, check_vma=False)
```

```python
import functools

import jax
import jax.numpy as jnp
from jax import lax
from jax.experimental import pallas as pl
from jax.experimental.pallas import tpu as pltpu
from jax.sharding import PartitionSpec as P

MESH = pl.DeviceIdType.MESH
F32 = jnp.float32
BF16 = jnp.bfloat16


def level(
    nb, nc, vol, w1h, w2h, wch, prh, skip, lift,
    x, y, w1, w2, wc, xc, con, rec, prj, acc1, acc2, tmp,
    loc, s1, r1, s2, r2, sp, rp, sw, rw, sf, rf, sg, rg, sc, rc, near,
):
    b = lax.axis_index("brick")
    c = lax.axis_index("chan")
    q = lax.rem(b, 2)
    slow = lax.rem(b + 2 * q - 1 + nb, nb)
    fast = lax.rem(b + 1 - 2 * q + nb, nb)
    below = lax.rem(b - 1 + nb, nb)
    above = lax.rem(b + 1, nb)
    nx = nc // 2
    row_of, place = c // nx, lax.rem(c, nx)

    def chan(d):
        return lax.rem(c + d, nc)

    loads = [
        pltpu.make_async_copy(vol.at[q], x.at[1, 1, pl.ds(1, 8)], loc.at[0]),
        pltpu.make_async_copy(vol.at[1 - q], x.at[1, 2, pl.ds(1, 8)], loc.at[1]),
        pltpu.make_async_copy(w1h, w1, loc.at[2]),
        pltpu.make_async_copy(prh, prj.at[c], loc.at[3]),
        pltpu.make_async_copy(wch, wc.at[:, pl.ds(pl.multiple_of(place * 64, 64), 64)], loc.at[4]),
        pltpu.make_async_copy(w2h, w2, loc.at[5]),
    ]
    for k in (0, 1):
        loads[k].start()

    right, left, across = chan(1), chan(nc - 1), chan(nx)
    barrier = pltpu.get_barrier_semaphore()
    for who in ((slow, c), (b, right), (b, left), (b, across), (fast, right), (fast, left), (fast, c)):
        pl.semaphore_signal(barrier, inc=1, device_id=who, device_id_type=MESH)
    loads[0].wait()
    loads[1].wait()
    pl.semaphore_wait(barrier, 7)

    def halo(buf, ss, rs):
        plans = [(1, 1 + i, 1, 0, 1 + i, (slow, c)) for i in range(8)]
        plans += [
            (1, 1, 1, 1, 9, (b, left)),
            (1, 8, 1, 1, 0, (b, right)),
            (2, 1, 1, 2, 9, (b, left)),
            (2, 8, 1, 2, 0, (b, right)),
            (2, 1, 8, 3, 1, (fast, c)),
            (2, 1, 1, 3, 9, (fast, left)),
            (2, 8, 1, 3, 0, (fast, right)),
            (1, 1, 1, 0, 9, (slow, left)),
            (1, 8, 1, 0, 0, (slow, right)),
        ]
        return [
            pltpu.make_async_remote_copy(
                buf.at[1, src, pl.ds(row, n)], buf.at[1, dst, pl.ds(to, n)],
                ss.at[i], rs.at[i], device_id=who, device_id_type=MESH,
            )
            for i, (src, row, n, dst, to, who) in enumerate(plans)
        ]

    def start(copies, *which):
        for k in which:
            copies[k].start()

    def arrived(copies, *which):
        for k in which:
            copies[k].wait_recv()

    first = halo(x, s1, r1)
    start(first, 12, 8, 9, 10, 11, 0, 1, 2, 3, 4, 5, 6, 7, 13, 14)
    for who in (right, left, across):
        pl.semaphore_signal(near, inc=1, device_id=(b, who), device_id_type=MESH)
    for k in (3, 2, 4, 5):
        loads[k].start()

    gifts = [
        pltpu.make_async_remote_copy(
            prj.at[block], prj.at[block], sp.at[i], rp.at[i],
            device_id=(b, row_of * nx + lax.rem(place + d, nx) if d else across), device_id_type=MESH,
        )
        for i, (block, d) in enumerate(
            [(c, 0)] + [(block, d) for d in range(1, nx) for block in (c, across)]
        )
    ]

    def shard(owner, core):
        return pl.ds(pl.multiple_of(owner * 64 + core * 32, 32), 32)

    def along(d):
        return lax.rem(place + d, nx)

    blocks = (pl.ds(0, 14), pl.ds(14, 13))

    def ring(slot, source, part, owner, to):
        return pltpu.make_async_remote_copy(
            source, wc.at[blocks[part], shard(owner, q)], sw.at[slot], rw.at[slot],
            device_id=(b, row_of * nx + to), device_id_type=MESH,
        )

    ahead, behind = along(1), along(nx - 1)
    mine = [wch.at[part, pl.ds(pl.multiple_of(q * 32, 32), 32)] for part in blocks]
    weights = [
        ring(0, mine[0], 0, place, ahead),
        ring(1, mine[1], 1, place, behind),
        ring(2, mine[1], 1, place, ahead),
        ring(3, mine[0], 0, place, behind),
        ring(4, wc.at[blocks[0], shard(behind, q)], 0, behind, ahead),
        ring(5, wc.at[blocks[1], shard(ahead, q)], 1, ahead, behind),
    ]
    passed = [
        pltpu.make_async_remote_copy(
            wc.at[:, shard(owner, q)], wc.at[:, shard(owner, q)], sf.at[d], rf.at[d],
            device_id=(fast, c), device_id_type=MESH,
        )
        for d, owner in enumerate((behind, ahead, along(nx // 2)))
    ]

    zero_row = jnp.zeros((1, 256), BF16)

    def spread(buf, p, row, v):
        buf[0, p, row] = jnp.concatenate([zero_row, v[:-1]], axis=0)
        buf[2, p, row] = jnp.concatenate([v[1:], zero_row], axis=0)

    def spread_rows(buf, p, start, n):
        def body(i, _):
            spread(buf, p, start + i, buf[1, p, start + i])
            return 0
        lax.fori_loop(0, n, body, 0, unroll=4)

    has_low, has_high = c > 0, c < nc - 1
    has_slow = jnp.logical_and(slow != b + nb - 1, slow != b + 1 - nb)

    def masked(buf, p, row, valid):
        v = jnp.where(valid, buf[1, p, row].astype(F32), 0.0).astype(BF16)
        buf[1, p, row] = v
        spread(buf, p, row, v)

    def edge_rows(buf, copies, u):
        arrived(copies, 8 + 2 * u, 9 + 2 * u)
        masked(buf, u + 1, 9, has_high)
        masked(buf, u + 1, 0, has_low)

    def slow_rows(buf, copies):
        arrived(copies, *range(8))
        spread_rows(buf, 0, 1, 8)

    def slow_corners(buf, copies):
        arrived(copies, 15, 16)
        masked(buf, 0, 0, has_low)
        masked(buf, 0, 9, has_high)

    def fast_halo(buf, copies):
        arrived(copies, 12, 13, 14)
        masked(buf, 3, 0, has_low)
        masked(buf, 3, 9, has_high)
        spread_rows(buf, 3, 1, 8)

    def taps(buf, w, u, i, row=0, n=8):
        lhs = jnp.concatenate(
            [
                buf[k, u + i, row + j : row + j + n].reshape(n * 64, 256)
                for j in range(3) for k in range(3)
            ],
            axis=1,
        )
        return jnp.dot(lhs, w[i + q * (2 - 2 * i)], preferred_element_type=F32)

    def slow_middle(acc, buf, w):
        acc[0, 64:448] += jnp.where(has_slow, taps(buf, w, 0, 0, 1, 6), 0.0)

    def slow_edges(acc, buf, w):
        lhs = jnp.concatenate(
            [
                jnp.concatenate([buf[k, 0, j], buf[k, 0, 7 + j]], axis=0)
                for j in range(3) for k in range(3)
            ],
            axis=1,
        )
        got = jnp.where(has_slow, jnp.dot(lhs, w[2 * q], preferred_element_type=F32), 0.0)
        acc[0, 0:64] += got[:64]
        acc[0, 448:512] += got[64:]

    def finish_one(u, start=0, n=8):
        def body(r, _):
            v = jnp.maximum(acc1[u, pl.ds(pl.multiple_of(r * 64, 64), 64)], 0.0).astype(BF16)
            y[1, u + 1, 1 + r] = v
            spread(y, u + 1, 1 + r, v)
            return 0
        lax.fori_loop(start, start + n, body, 0)

    pl.semaphore_wait(near, 3)
    start(first, 15, 16)
    start(weights, 0, 1, 2, 3)
    loads[3].wait()
    start(gifts, 0)
    spread_rows(x, 1, 1, 8)
    spread_rows(x, 2, 1, 8)
    edge_rows(x, first, 0)
    edge_rows(x, first, 1)
    loads[2].wait()
    acc1[1] = taps(x, w1, 1, 0) + taps(x, w1, 1, 1)
    fast_halo(x, first)
    acc1[1] += taps(x, w1, 1, 2)
    finish_one(1)
    second = halo(y, s2, r2)
    start(second, 12, 10, 11, 13, 14)
    acc1[0] = taps(x, w1, 0, 1) + taps(x, w1, 0, 2)
    arrived(weights, 0, 1)
    start(weights, 4, 5)
    slow_rows(x, first)
    slow_middle(acc1, x, w1)
    finish_one(0, 1, 6)
    start(second, 1, 2, 3, 4, 5, 6)
    slow_corners(x, first)
    slow_edges(acc1, x, w1)
    finish_one(0, 0, 1)
    finish_one(0, 7, 1)
    start(second, 15, 16, 0, 7, 8, 9)

    loads[5].wait()
    edge_rows(y, second, 1)
    acc2[1] = taps(y, w2, 1, 1)
    acc2[0] = taps(y, w2, 0, 2)
    fast_halo(y, second)
    acc2[1] += taps(y, w2, 1, 2)
    edge_rows(y, second, 0)
    acc2[1] += taps(y, w2, 1, 0)
    acc2[0] += taps(y, w2, 0, 1)
    loads[4].wait()
    arrived(weights, 2, 3)
    start(passed, 0, 1)
    slow_rows(y, second)
    slow_middle(acc2, y, w2)
    slow_corners(y, second)
    slow_edges(acc2, y, w2)
    def pool(r, _):
        total = jnp.zeros((64, 256), F32)
        for u in range(2):
            for s in range(2):
                rows = pl.ds(pl.multiple_of(r * 128 + s * 64, 64), 64)
                v = jnp.maximum(acc2[u, rows], 0.0).astype(BF16)
                skip[u + q * (1 - 2 * u), 2 * r + s] = v
                total = total + v.astype(F32)
        halves = []
        for h in range(2):
            tmp[r, h] = total[:, h * 128 : h * 128 + 128]
            even = tmp[r, h, pl.ds(0, 32, stride=2)]
            odd = tmp[r, h, pl.ds(1, 32, stride=2)]
            halves.append(((even + odd) * 0.125).astype(BF16))
        xc[1, row_of, 1 + r] = jnp.concatenate(halves, axis=1)
        return 0
    lax.fori_loop(0, 4, pool, 0, unroll=2)

    partner = across
    shares = [
        pltpu.make_async_remote_copy(
            xc.at[1, row_of, pl.ds(row, n)], xc.at[1, slot, pl.ds(to, n)],
            sg.at[i], rg.at[i], device_id=(b, who), device_id_type=MESH,
        )
        for i, (row, n, slot, to, who) in enumerate(
            [
                (1, 4, row_of, 1, partner),
                (4, 1, chan(1) // nx, 0, chan(1)),
                (4, 1, chan(1) // nx, 0, chan(1 + nx)),
                (1, 1, chan(nc - 1) // nx, 5, chan(nc - 1)),
                (1, 1, chan(nc - 1) // nx, 5, chan(nx - 1)),
            ]
        )
    ]
    for share in shares:
        share.start()
    arrived(gifts, 0)
    start(gifts, *range(1, 2 * nx - 1))
    arrived(weights, 4, 5)
    start(passed, 2)
    for share in shares:
        share.wait_recv()

    def widen(h, r, v):
        xc[0, h, r] = jnp.concatenate([zero_row, v[:-1]], axis=0)
        xc[2, h, r] = jnp.concatenate([v[1:], zero_row], axis=0)

    for h in range(2):
        block = h * nx + place
        for r, valid in ((0, block > 0), (5, block < nc - 1)):
            v = jnp.where(valid, xc[1, h, r].astype(F32), 0.0).astype(BF16)
            xc[1, h, r] = v
            widen(h, r, v)

        def coarse_row(r, _):
            widen(h, r, xc[1, h, r])
            return 0
        lax.fori_loop(1, 5, coarse_row, 0, unroll=4)
    arrived(passed, 0, 1, 2)

    parts = []
    for role, (tap, brick) in enumerate(((2 - 2 * q, slow), (1, b), (2 * q, fast))):
        lhs = jnp.concatenate(
            [xc[k, :, j : j + 4].reshape(256, 256) for j in range(3) for k in range(3)], axis=1
        )
        rhs = jnp.concatenate([wc[tap * 9 + jk] for jk in range(9)], axis=1)
        got = lax.dot_general(lhs, rhs, (((1,), (1,)), ((), ())), preferred_element_type=F32)
        con[role] = got.astype(BF16).reshape(2, 128, 256)
        for t, slot, who in ((0, row_of, c), (1, 1 - row_of, partner)):
            if role == 1 and t == 0:
                rec[1, row_of] = con[1, row_of]
                continue
            copy = pltpu.make_async_remote_copy(
                con.at[role, slot], rec.at[role, row_of], sc.at[role, t], rc.at[role, t],
                device_id=(brick, who), device_id_type=MESH,
            )
            copy.start()
            parts.append(copy)
    arrived(gifts, *range(1, 2 * nx - 1))
    for part in parts:
        part.wait_recv()

    cols = []
    for h in range(2):
        total = rec[1, h].astype(F32) + rec[2, h].astype(F32)
        total = total + jnp.where(has_slow, rec[0, h].astype(F32), 0.0)
        cols.append(jnp.maximum(total, 0.0).astype(BF16))
    lifted = jnp.dot(
        jnp.concatenate(cols, axis=1), prj[...].reshape(nc * 64, 256), preferred_element_type=F32
    )
    lift[...] = lifted.reshape(4, 32, 256)

    for copy in first + second + gifts + shares + parts + weights + passed:
        copy.wait_send()


def merge(skip, lift, out, cells, done, rows, tmp, come, go):
    whole = pltpu.make_async_copy(lift, rows, come.at[8])
    whole.start()
    loads = [
        pltpu.make_async_copy(skip.at[u, pl.ds(2 * r, 2)], cells.at[u, r], come.at[2 * r + u])
        for r in range(4) for u in range(2)
    ]
    for load in loads:
        load.start()
    whole.wait()
    stores = []
    for r in range(4):
        for h in range(2):
            piece = rows[r, :, h * 128 : h * 128 + 128]
            tmp[r, h, pl.ds(0, 32, stride=2)] = piece
            tmp[r, h, pl.ds(1, 32, stride=2)] = piece
        wide = jnp.concatenate([tmp[r, 0], tmp[r, 1]], axis=1)
        for u in range(2):
            loads[2 * r + u].wait()
            for s in range(2):
                done[u, r, s] = (cells[u, r, s].astype(F32) + wide).astype(BF16)
            store = pltpu.make_async_copy(done.at[u, r], out.at[u, pl.ds(2 * r, 2)], go.at[2 * r + u])
            store.start()
            stores.append(store)
    for store in stores:
        store.wait()


def shards(nb, nc, volume, first_weight, second_weight, coarse_weight, projection):
    dma = pltpu.SemaphoreType.DMA
    skip, lift = pl.pallas_call(
        functools.partial(level, nb, nc),
        out_shape=(
            jax.ShapeDtypeStruct(volume.shape, BF16),
            jax.ShapeDtypeStruct((4, 32, 256), F32),
        ),
        in_specs=[pl.BlockSpec(memory_space=pl.ANY)] * 5,
        out_specs=(pl.BlockSpec(memory_space=pltpu.VMEM),) * 2,
        scratch_shapes=[
            pltpu.VMEM((3, 4, 10, 64, 256), BF16),
            pltpu.VMEM((3, 4, 10, 64, 256), BF16),
            pltpu.VMEM((3, 2304, 256), BF16),
            pltpu.VMEM((3, 2304, 256), BF16),
            pltpu.VMEM((27, 256, 256), BF16),
            pltpu.VMEM((3, 2, 6, 32, 256), BF16),
            pltpu.VMEM((3, 2, 128, 256), BF16),
            pltpu.VMEM((3, 2, 128, 256), BF16),
            pltpu.VMEM((nc, 64, 256), BF16),
            pltpu.VMEM((2, 512, 256), F32),
            pltpu.VMEM((2, 512, 256), F32),
            pltpu.VMEM((4, 2, 64, 128), F32),
            dma((6,)),
            dma((17,)),
            dma((17,)),
            dma((17,)),
            dma((17,)),
            dma((nc,)),
            dma((nc,)),
            dma((6,)),
            dma((6,)),
            dma((3,)),
            dma((3,)),
            dma((5,)),
            dma((5,)),
            dma((3, 2)),
            dma((3, 2)),
            pltpu.SemaphoreType.REGULAR,
        ],
        compiler_params=pltpu.CompilerParams(
            collective_id=0, has_side_effects=True, vmem_limit_bytes=56 << 20
        ),
        name="level",
    )(
        volume,
        first_weight.reshape(3, 2304, 256),
        second_weight.reshape(3, 2304, 256),
        jnp.swapaxes(coarse_weight, 3, 4).reshape(27, 64, 256),
        projection,
    )
    return pl.pallas_call(
        merge,
        out_shape=jax.ShapeDtypeStruct(volume.shape, BF16),
        in_specs=[pl.BlockSpec(memory_space=pl.ANY)] * 2,
        out_specs=pl.BlockSpec(memory_space=pl.ANY),
        scratch_shapes=[
            pltpu.VMEM((2, 4, 2, 64, 256), BF16),
            pltpu.VMEM((2, 4, 2, 64, 256), BF16),
            pltpu.VMEM((4, 32, 256), F32),
            pltpu.VMEM((4, 2, 64, 128), F32),
            dma((9,)),
            dma((8,)),
        ],
        compiler_params=pltpu.CompilerParams(vmem_limit_bytes=63 << 20),
        name="merge",
    )(skip, lift)


def solution(mesh):
    in_specs = (
        P("brick", "chan", None, None),
        P(),
        P(),
        P(None, None, None, None, "chan"),
        P("chan", None),
    )
    out_specs = P("brick", "chan", None, None)
    body = functools.partial(shards, mesh.shape["brick"], mesh.shape["chan"])
    return jax.shard_map(body, mesh=mesh, in_specs=in_specs, out_specs=out_specs, check_vma=False)
```

```python
import functools

import jax
import jax.numpy as jnp
from jax import lax
from jax.experimental import pallas as pl
from jax.experimental.pallas import tpu as pltpu
from jax.sharding import PartitionSpec as P

MESH = pl.DeviceIdType.MESH
F32 = jnp.float32
BF16 = jnp.bfloat16


def level(
    nb, nc, vol, w1h, w2h, wch, prh, skip, lift,
    x, y, w1, w2, wc, xc, con, rec, prj, acc1, acc2, tmp,
    loc, s1, r1, s2, r2, sp, rp, sw, rw, sf, rf, sg, rg, sc, rc, near,
):
    b = lax.axis_index("brick")
    c = lax.axis_index("chan")
    q = lax.rem(b, 2)
    slow = lax.rem(b + 2 * q - 1 + nb, nb)
    fast = lax.rem(b + 1 - 2 * q + nb, nb)
    below = lax.rem(b - 1 + nb, nb)
    above = lax.rem(b + 1, nb)
    nx = nc // 2
    row_of, place = c // nx, lax.rem(c, nx)

    def chan(d):
        return lax.rem(c + d, nc)

    loads = [
        pltpu.make_async_copy(vol.at[q], x.at[1, 1, pl.ds(1, 8)], loc.at[0]),
        pltpu.make_async_copy(vol.at[1 - q], x.at[1, 2, pl.ds(1, 8)], loc.at[1]),
        pltpu.make_async_copy(w1h, w1, loc.at[2]),
        pltpu.make_async_copy(prh, prj.at[c], loc.at[3]),
        pltpu.make_async_copy(wch, wc.at[:, pl.ds(pl.multiple_of(place * 64, 64), 64)], loc.at[4]),
        pltpu.make_async_copy(w2h, w2, loc.at[5]),
    ]
    for k in (0, 1):
        loads[k].start()

    right, left, across = chan(1), chan(nc - 1), chan(nx)
    barrier = pltpu.get_barrier_semaphore()
    for who in ((slow, c), (b, right), (b, left), (b, across), (fast, right), (fast, left), (fast, c)):
        pl.semaphore_signal(barrier, inc=1, device_id=who, device_id_type=MESH)
    loads[0].wait()
    loads[1].wait()
    pl.semaphore_wait(barrier, 7)

    def halo(buf, ss, rs):
        plans = [(1, 1 + i, 1, 0, 1 + i, (slow, c)) for i in range(8)]
        plans += [
            (1, 1, 1, 1, 9, (b, left)),
            (1, 8, 1, 1, 0, (b, right)),
            (2, 1, 1, 2, 9, (b, left)),
            (2, 8, 1, 2, 0, (b, right)),
            (2, 1, 8, 3, 1, (fast, c)),
            (2, 1, 1, 3, 9, (fast, left)),
            (2, 8, 1, 3, 0, (fast, right)),
            (1, 1, 1, 0, 9, (slow, left)),
            (1, 8, 1, 0, 0, (slow, right)),
        ]
        return [
            pltpu.make_async_remote_copy(
                buf.at[1, src, pl.ds(row, n)], buf.at[1, dst, pl.ds(to, n)],
                ss.at[i], rs.at[i], device_id=who, device_id_type=MESH,
            )
            for i, (src, row, n, dst, to, who) in enumerate(plans)
        ]

    def start(copies, *which):
        for k in which:
            copies[k].start()

    def arrived(copies, *which):
        for k in which:
            copies[k].wait_recv()

    first = halo(x, s1, r1)
    start(first, 12, 8, 9, 10, 11, 0, 1, 2, 3, 4, 5, 6, 7, 13, 14)
    for who in (right, left, across):
        pl.semaphore_signal(near, inc=1, device_id=(b, who), device_id_type=MESH)
    for k in (3, 2, 4, 5):
        loads[k].start()

    gifts = [
        pltpu.make_async_remote_copy(
            prj.at[block], prj.at[block], sp.at[i], rp.at[i],
            device_id=(b, row_of * nx + lax.rem(place + d, nx) if d else across), device_id_type=MESH,
        )
        for i, (block, d) in enumerate(
            [(c, 0)] + [(block, d) for d in range(1, nx) for block in (c, across)]
        )
    ]

    def shard(owner, core):
        return pl.ds(pl.multiple_of(owner * 64 + core * 32, 32), 32)

    def along(d):
        return lax.rem(place + d, nx)

    blocks = (pl.ds(0, 14), pl.ds(14, 13))

    def ring(slot, source, part, owner, to):
        return pltpu.make_async_remote_copy(
            source, wc.at[blocks[part], shard(owner, q)], sw.at[slot], rw.at[slot],
            device_id=(b, row_of * nx + to), device_id_type=MESH,
        )

    ahead, behind = along(1), along(nx - 1)
    mine = [wch.at[part, pl.ds(pl.multiple_of(q * 32, 32), 32)] for part in blocks]
    weights = [
        ring(0, mine[0], 0, place, ahead),
        ring(1, mine[1], 1, place, behind),
        ring(2, mine[1], 1, place, ahead),
        ring(3, mine[0], 0, place, behind),
        ring(4, wc.at[blocks[0], shard(behind, q)], 0, behind, ahead),
        ring(5, wc.at[blocks[1], shard(ahead, q)], 1, ahead, behind),
    ]
    passed = [
        pltpu.make_async_remote_copy(
            wc.at[:, shard(owner, q)], wc.at[:, shard(owner, q)], sf.at[d], rf.at[d],
            device_id=(fast, c), device_id_type=MESH,
        )
        for d, owner in enumerate((behind, ahead, along(nx // 2)))
    ]

    zero_row = jnp.zeros((1, 256), BF16)

    def spread(buf, p, row, v):
        buf[0, p, row] = jnp.concatenate([zero_row, v[:-1]], axis=0)
        buf[2, p, row] = jnp.concatenate([v[1:], zero_row], axis=0)

    def spread_rows(buf, p, start, n):
        def body(i, _):
            spread(buf, p, start + i, buf[1, p, start + i])
            return 0
        lax.fori_loop(0, n, body, 0, unroll=4)

    has_low, has_high = c > 0, c < nc - 1
    has_slow = jnp.logical_and(slow != b + nb - 1, slow != b + 1 - nb)

    def masked(buf, p, row, valid):
        v = jnp.where(valid, buf[1, p, row].astype(F32), 0.0).astype(BF16)
        buf[1, p, row] = v
        spread(buf, p, row, v)

    def edge_rows(buf, copies, u):
        arrived(copies, 8 + 2 * u, 9 + 2 * u)
        masked(buf, u + 1, 9, has_high)
        masked(buf, u + 1, 0, has_low)

    def slow_rows(buf, copies):
        arrived(copies, *range(8))
        spread_rows(buf, 0, 1, 8)

    def slow_corners(buf, copies):
        arrived(copies, 15, 16)
        masked(buf, 0, 0, has_low)
        masked(buf, 0, 9, has_high)

    def fast_halo(buf, copies):
        arrived(copies, 12, 13, 14)
        masked(buf, 3, 0, has_low)
        masked(buf, 3, 9, has_high)
        spread_rows(buf, 3, 1, 8)

    def taps(buf, w, u, i, row=0, n=8):
        lhs = jnp.concatenate(
            [
                buf[k, u + i, row + j : row + j + n].reshape(n * 64, 256)
                for j in range(3) for k in range(3)
            ],
            axis=1,
        )
        return jnp.dot(lhs, w[i + q * (2 - 2 * i)], preferred_element_type=F32)

    def slow_middle(acc, buf, w):
        acc[0, 64:448] += jnp.where(has_slow, taps(buf, w, 0, 0, 1, 6), 0.0)

    def slow_edges(acc, buf, w):
        lhs = jnp.concatenate(
            [
                jnp.concatenate([buf[k, 0, j], buf[k, 0, 7 + j]], axis=0)
                for j in range(3) for k in range(3)
            ],
            axis=1,
        )
        got = jnp.where(has_slow, jnp.dot(lhs, w[2 * q], preferred_element_type=F32), 0.0)
        acc[0, 0:64] += got[:64]
        acc[0, 448:512] += got[64:]

    def finish_one(u, start=0, n=8):
        def body(r, _):
            v = jnp.maximum(acc1[u, pl.ds(pl.multiple_of(r * 64, 64), 64)], 0.0).astype(BF16)
            y[1, u + 1, 1 + r] = v
            spread(y, u + 1, 1 + r, v)
            return 0
        lax.fori_loop(start, start + n, body, 0)

    pl.semaphore_wait(near, 3)
    start(first, 15, 16)
    start(weights, 0, 1, 2, 3)
    loads[3].wait()
    start(gifts, 0)
    spread_rows(x, 1, 1, 8)
    spread_rows(x, 2, 1, 8)
    edge_rows(x, first, 0)
    edge_rows(x, first, 1)
    loads[2].wait()
    acc1[1] = taps(x, w1, 1, 0) + taps(x, w1, 1, 1)
    fast_halo(x, first)
    acc1[1] += taps(x, w1, 1, 2)
    finish_one(1)
    second = halo(y, s2, r2)
    start(second, 12, 10, 11, 13, 14)
    acc1[0] = taps(x, w1, 0, 1) + taps(x, w1, 0, 2)
    arrived(weights, 0, 1)
    start(weights, 4, 5)
    slow_rows(x, first)
    slow_middle(acc1, x, w1)
    finish_one(0, 1, 6)
    start(second, 1, 2, 3, 4, 5, 6)
    slow_corners(x, first)
    slow_edges(acc1, x, w1)
    finish_one(0, 0, 1)
    finish_one(0, 7, 1)
    start(second, 15, 16, 0, 7, 8, 9)

    loads[5].wait()
    edge_rows(y, second, 1)
    acc2[1] = taps(y, w2, 1, 1)
    acc2[0] = taps(y, w2, 0, 2)
    fast_halo(y, second)
    acc2[1] += taps(y, w2, 1, 2)
    edge_rows(y, second, 0)
    acc2[1] += taps(y, w2, 1, 0)
    acc2[0] += taps(y, w2, 0, 1)
    loads[4].wait()
    arrived(weights, 2, 3)
    start(passed, 0, 1)
    slow_rows(y, second)
    slow_middle(acc2, y, w2)
    slow_corners(y, second)
    slow_edges(acc2, y, w2)
    def pool(r, _):
        total = jnp.zeros((64, 256), F32)
        for u in range(2):
            for s in range(2):
                rows = pl.ds(pl.multiple_of(r * 128 + s * 64, 64), 64)
                v = jnp.maximum(acc2[u, rows], 0.0).astype(BF16)
                skip[u + q * (1 - 2 * u), 2 * r + s] = v
                total = total + v.astype(F32)
        halves = []
        for h in range(2):
            tmp[r, h] = total[:, h * 128 : h * 128 + 128]
            even = tmp[r, h, pl.ds(0, 32, stride=2)]
            odd = tmp[r, h, pl.ds(1, 32, stride=2)]
            halves.append(((even + odd) * 0.125).astype(BF16))
        xc[1, row_of, 1 + r] = jnp.concatenate(halves, axis=1)
        return 0
    lax.fori_loop(0, 4, pool, 0, unroll=2)

    partner = across
    shares = [
        pltpu.make_async_remote_copy(
            xc.at[1, row_of, pl.ds(row, n)], xc.at[1, slot, pl.ds(to, n)],
            sg.at[i], rg.at[i], device_id=(b, who), device_id_type=MESH,
        )
        for i, (row, n, slot, to, who) in enumerate(
            [
                (1, 4, row_of, 1, partner),
                (4, 1, chan(1) // nx, 0, chan(1)),
                (4, 1, chan(1) // nx, 0, chan(1 + nx)),
                (1, 1, chan(nc - 1) // nx, 5, chan(nc - 1)),
                (1, 1, chan(nc - 1) // nx, 5, chan(nx - 1)),
            ]
        )
    ]
    for share in shares:
        share.start()
    arrived(gifts, 0)
    start(gifts, *range(1, 2 * nx - 1))
    arrived(weights, 4, 5)
    start(passed, 2)
    for share in shares:
        share.wait_recv()

    def widen(h, r, v):
        xc[0, h, r] = jnp.concatenate([zero_row, v[:-1]], axis=0)
        xc[2, h, r] = jnp.concatenate([v[1:], zero_row], axis=0)

    for h in range(2):
        block = h * nx + place
        for r, valid in ((0, block > 0), (5, block < nc - 1)):
            v = jnp.where(valid, xc[1, h, r].astype(F32), 0.0).astype(BF16)
            xc[1, h, r] = v
            widen(h, r, v)

        def coarse_row(r, _):
            widen(h, r, xc[1, h, r])
            return 0
        lax.fori_loop(1, 5, coarse_row, 0, unroll=4)
    arrived(passed, 0, 1, 2)

    parts = []
    for role, (tap, brick) in enumerate(((2 - 2 * q, slow), (1, b), (2 * q, fast))):
        lhs = jnp.concatenate(
            [xc[k, :, j : j + 4].reshape(256, 256) for j in range(3) for k in range(3)], axis=1
        )
        rhs = jnp.concatenate([wc[tap * 9 + jk] for jk in range(9)], axis=1)
        got = lax.dot_general(lhs, rhs, (((1,), (1,)), ((), ())), preferred_element_type=F32)
        con[role] = got.astype(BF16).reshape(2, 128, 256)
        for t, slot, who in ((0, row_of, c), (1, 1 - row_of, partner)):
            if role == 1 and t == 0:
                rec[1, row_of] = con[1, row_of]
                continue
            copy = pltpu.make_async_remote_copy(
                con.at[role, slot], rec.at[role, row_of], sc.at[role, t], rc.at[role, t],
                device_id=(brick, who), device_id_type=MESH,
            )
            copy.start()
            parts.append(copy)
    arrived(gifts, *range(1, 2 * nx - 1))
    for part in parts:
        part.wait_recv()

    cols = []
    for h in range(2):
        total = rec[1, h].astype(F32) + rec[2, h].astype(F32)
        total = total + jnp.where(has_slow, rec[0, h].astype(F32), 0.0)
        cols.append(jnp.maximum(total, 0.0).astype(BF16))
    lifted = jnp.dot(
        jnp.concatenate(cols, axis=1), prj[...].reshape(nc * 64, 256), preferred_element_type=F32
    )
    lift[...] = lifted.reshape(4, 32, 256)

    for copy in first + second + gifts + shares + parts + weights + passed:
        copy.wait_send()


def merge(skip, lift, out, cells, done, rows, tmp, come, go):
    whole = pltpu.make_async_copy(lift, rows, come.at[8])
    whole.start()
    loads = [
        pltpu.make_async_copy(skip.at[u, pl.ds(2 * r, 2)], cells.at[u, r], come.at[2 * r + u])
        for r in range(4) for u in range(2)
    ]
    for load in loads:
        load.start()
    whole.wait()
    stores = []
    for r in range(4):
        for h in range(2):
            piece = rows[r, :, h * 128 : h * 128 + 128]
            tmp[r, h, pl.ds(0, 32, stride=2)] = piece
            tmp[r, h, pl.ds(1, 32, stride=2)] = piece
        wide = jnp.concatenate([tmp[r, 0], tmp[r, 1]], axis=1)
        for u in range(2):
            loads[2 * r + u].wait()
            for s in range(2):
                done[u, r, s] = (cells[u, r, s].astype(F32) + wide).astype(BF16)
            store = pltpu.make_async_copy(done.at[u, r], out.at[u, pl.ds(2 * r, 2)], go.at[2 * r + u])
            store.start()
            stores.append(store)
    for store in stores:
        store.wait()


def shards(nb, nc, volume, first_weight, second_weight, coarse_weight, projection):
    dma = pltpu.SemaphoreType.DMA
    skip, lift = pl.pallas_call(
        functools.partial(level, nb, nc),
        out_shape=(
            jax.ShapeDtypeStruct(volume.shape, BF16),
            jax.ShapeDtypeStruct((4, 32, 256), F32),
        ),
        in_specs=[pl.BlockSpec(memory_space=pl.ANY)] * 5,
        out_specs=(pl.BlockSpec(memory_space=pltpu.VMEM),) * 2,
        scratch_shapes=[
            pltpu.VMEM((3, 4, 10, 64, 256), BF16),
            pltpu.VMEM((3, 4, 10, 64, 256), BF16),
            pltpu.VMEM((3, 2304, 256), BF16),
            pltpu.VMEM((3, 2304, 256), BF16),
            pltpu.VMEM((27, 256, 256), BF16),
            pltpu.VMEM((3, 2, 6, 32, 256), BF16),
            pltpu.VMEM((3, 2, 128, 256), BF16),
            pltpu.VMEM((3, 2, 128, 256), BF16),
            pltpu.VMEM((nc, 64, 256), BF16),
            pltpu.VMEM((2, 512, 256), F32),
            pltpu.VMEM((2, 512, 256), F32),
            pltpu.VMEM((4, 2, 64, 128), F32),
            dma((6,)),
            dma((17,)),
            dma((17,)),
            dma((17,)),
            dma((17,)),
            dma((nc,)),
            dma((nc,)),
            dma((6,)),
            dma((6,)),
            dma((3,)),
            dma((3,)),
            dma((5,)),
            dma((5,)),
            dma((3, 2)),
            dma((3, 2)),
            pltpu.SemaphoreType.REGULAR,
        ],
        compiler_params=pltpu.CompilerParams(
            collective_id=0, has_side_effects=True, vmem_limit_bytes=50 << 20
        ),
        name="level",
    )(
        *(
            pltpu.with_memory_space_constraint(v, pltpu.HBM)
            for v in (
                volume,
                first_weight.reshape(3, 2304, 256),
                second_weight.reshape(3, 2304, 256),
                jnp.swapaxes(coarse_weight, 3, 4).reshape(27, 64, 256),
                projection,
            )
        )
    )
    return pl.pallas_call(
        merge,
        out_shape=jax.ShapeDtypeStruct(volume.shape, BF16),
        in_specs=[pl.BlockSpec(memory_space=pl.ANY)] * 2,
        out_specs=pl.BlockSpec(memory_space=pl.ANY),
        scratch_shapes=[
            pltpu.VMEM((2, 4, 2, 64, 256), BF16),
            pltpu.VMEM((2, 4, 2, 64, 256), BF16),
            pltpu.VMEM((4, 32, 256), F32),
            pltpu.VMEM((4, 2, 64, 128), F32),
            dma((9,)),
            dma((8,)),
        ],
        compiler_params=pltpu.CompilerParams(vmem_limit_bytes=8 << 20),
        name="merge",
    )(skip, lift)


def solution(mesh):
    in_specs = (
        P("brick", "chan", None, None),
        P(),
        P(),
        P(None, None, None, None, "chan"),
        P("chan", None),
    )
    out_specs = P("brick", "chan", None, None)
    body = functools.partial(shards, mesh.shape["brick"], mesh.shape["chan"])
    return jax.shard_map(body, mesh=mesh, in_specs=in_specs, out_specs=out_specs, check_vma=False)
```

```python
import functools

import jax
import jax.numpy as jnp
from jax import lax
from jax.experimental import pallas as pl
from jax.experimental.pallas import tpu as pltpu
from jax.sharding import PartitionSpec as P

MESH = pl.DeviceIdType.MESH
F32 = jnp.float32
BF16 = jnp.bfloat16


def level(
    nb, nc, vol, w1h, w2h, wch, prh, skip, lift,
    x, y, w1, w2, wc, xc, con, rec, prj, acc1, acc2, tmp,
    loc, s1, r1, s2, r2, sp, rp, sw, rw, sf, rf, sg, rg, sc, rc, near,
):
    b = lax.axis_index("brick")
    c = lax.axis_index("chan")
    q = lax.rem(b, 2)
    slow = lax.rem(b + 2 * q - 1 + nb, nb)
    fast = lax.rem(b + 1 - 2 * q + nb, nb)
    below = lax.rem(b - 1 + nb, nb)
    above = lax.rem(b + 1, nb)
    nx = nc // 2
    row_of, place = c // nx, lax.rem(c, nx)

    def chan(d):
        return lax.rem(c + d, nc)

    loads = [
        pltpu.make_async_copy(vol.at[q], x.at[1, 1, pl.ds(1, 8)], loc.at[0]),
        pltpu.make_async_copy(vol.at[1 - q], x.at[1, 2, pl.ds(1, 8)], loc.at[1]),
        pltpu.make_async_copy(w1h, w1, loc.at[2]),
        pltpu.make_async_copy(prh, prj.at[c], loc.at[3]),
        pltpu.make_async_copy(wch, wc.at[:, pl.ds(pl.multiple_of(place * 64, 64), 64)], loc.at[4]),
        pltpu.make_async_copy(w2h, w2, loc.at[5]),
    ]
    for k in (0, 1):
        loads[k].start()

    right, left, across = chan(1), chan(nc - 1), chan(nx)
    barrier = pltpu.get_barrier_semaphore()
    for who in ((slow, c), (b, right), (b, left), (b, across), (fast, right), (fast, left), (fast, c)):
        pl.semaphore_signal(barrier, inc=1, device_id=who, device_id_type=MESH)
    loads[0].wait()
    loads[1].wait()
    pl.semaphore_wait(barrier, 7)

    def halo(buf, ss, rs):
        plans = [(1, 1 + i, 1, 0, 1 + i, (slow, c)) for i in range(8)]
        plans += [
            (1, 1, 1, 1, 9, (b, left)),
            (1, 8, 1, 1, 0, (b, right)),
            (2, 1, 1, 2, 9, (b, left)),
            (2, 8, 1, 2, 0, (b, right)),
            (2, 1, 8, 3, 1, (fast, c)),
            (2, 1, 1, 3, 9, (fast, left)),
            (2, 8, 1, 3, 0, (fast, right)),
            (1, 1, 1, 0, 9, (slow, left)),
            (1, 8, 1, 0, 0, (slow, right)),
        ]
        return [
            pltpu.make_async_remote_copy(
                buf.at[1, src, pl.ds(row, n)], buf.at[1, dst, pl.ds(to, n)],
                ss.at[i], rs.at[i], device_id=who, device_id_type=MESH,
            )
            for i, (src, row, n, dst, to, who) in enumerate(plans)
        ]

    def start(copies, *which):
        for k in which:
            copies[k].start()

    def arrived(copies, *which):
        for k in which:
            copies[k].wait_recv()

    first = halo(x, s1, r1)
    start(first, 12, 8, 9, 10, 11, 0, 1, 2, 3, 4, 5, 6, 7, 13, 14)
    for who in (right, left, across):
        pl.semaphore_signal(near, inc=1, device_id=(b, who), device_id_type=MESH)
    for k in (3, 2, 4, 5):
        loads[k].start()

    gifts = [
        pltpu.make_async_remote_copy(
            prj.at[block], prj.at[block], sp.at[i], rp.at[i],
            device_id=(b, row_of * nx + lax.rem(place + d, nx) if d else across), device_id_type=MESH,
        )
        for i, (block, d) in enumerate(
            [(c, 0)] + [(block, d) for d in range(1, nx) for block in (c, across)]
        )
    ]

    def shard(owner, core):
        return pl.ds(pl.multiple_of(owner * 64 + core * 32, 32), 32)

    def along(d):
        return lax.rem(place + d, nx)

    blocks = (pl.ds(0, 14), pl.ds(14, 13))

    def ring(slot, source, part, owner, to):
        return pltpu.make_async_remote_copy(
            source, wc.at[blocks[part], shard(owner, q)], sw.at[slot], rw.at[slot],
            device_id=(b, row_of * nx + to), device_id_type=MESH,
        )

    ahead, behind = along(1), along(nx - 1)
    mine = [wch.at[part, pl.ds(pl.multiple_of(q * 32, 32), 32)] for part in blocks]
    weights = [
        ring(0, mine[0], 0, place, ahead),
        ring(1, mine[1], 1, place, behind),
        ring(2, mine[1], 1, place, ahead),
        ring(3, mine[0], 0, place, behind),
        ring(4, wc.at[blocks[0], shard(behind, q)], 0, behind, ahead),
        ring(5, wc.at[blocks[1], shard(ahead, q)], 1, ahead, behind),
    ]
    passed = [
        pltpu.make_async_remote_copy(
            wc.at[:, shard(owner, q)], wc.at[:, shard(owner, q)], sf.at[d], rf.at[d],
            device_id=(fast, c), device_id_type=MESH,
        )
        for d, owner in enumerate((behind, ahead, along(nx // 2)))
    ]

    zero_row = jnp.zeros((1, 256), BF16)

    def spread(buf, p, row, v):
        buf[0, p, row] = jnp.concatenate([zero_row, v[:-1]], axis=0)
        buf[2, p, row] = jnp.concatenate([v[1:], zero_row], axis=0)

    def spread_rows(buf, p, start, n):
        def body(i, _):
            spread(buf, p, start + i, buf[1, p, start + i])
            return 0
        lax.fori_loop(0, n, body, 0, unroll=4)

    has_low, has_high = c > 0, c < nc - 1
    has_slow = jnp.logical_and(slow != b + nb - 1, slow != b + 1 - nb)

    def masked(buf, p, row, valid):
        v = jnp.where(valid, buf[1, p, row].astype(F32), 0.0).astype(BF16)
        buf[1, p, row] = v
        spread(buf, p, row, v)

    def edge_rows(buf, copies, u):
        arrived(copies, 8 + 2 * u, 9 + 2 * u)
        masked(buf, u + 1, 9, has_high)
        masked(buf, u + 1, 0, has_low)

    def slow_rows(buf, copies):
        arrived(copies, *range(8))
        spread_rows(buf, 0, 1, 8)

    def slow_corners(buf, copies):
        arrived(copies, 15, 16)
        masked(buf, 0, 0, has_low)
        masked(buf, 0, 9, has_high)

    def fast_halo(buf, copies):
        arrived(copies, 12, 13, 14)
        masked(buf, 3, 0, has_low)
        masked(buf, 3, 9, has_high)
        spread_rows(buf, 3, 1, 8)

    def taps(buf, w, u, i, row=0, n=8):
        lhs = jnp.concatenate(
            [
                buf[k, u + i, row + j : row + j + n].reshape(n * 64, 256)
                for j in range(3) for k in range(3)
            ],
            axis=1,
        )
        return jnp.dot(lhs, w[i + q * (2 - 2 * i)], preferred_element_type=F32)

    def slow_middle(acc, buf, w):
        acc[0, 64:448] += jnp.where(has_slow, taps(buf, w, 0, 0, 1, 6), 0.0)

    def slow_edges(acc, buf, w):
        lhs = jnp.concatenate(
            [
                jnp.concatenate([buf[k, 0, j], buf[k, 0, 7 + j]], axis=0)
                for j in range(3) for k in range(3)
            ],
            axis=1,
        )
        got = jnp.where(has_slow, jnp.dot(lhs, w[2 * q], preferred_element_type=F32), 0.0)
        acc[0, 0:64] += got[:64]
        acc[0, 448:512] += got[64:]

    def finish_one(u, start=0, n=8):
        def body(r, _):
            v = jnp.maximum(acc1[u, pl.ds(pl.multiple_of(r * 64, 64), 64)], 0.0).astype(BF16)
            y[1, u + 1, 1 + r] = v
            spread(y, u + 1, 1 + r, v)
            return 0
        lax.fori_loop(start, start + n, body, 0)

    pl.semaphore_wait(near, 3)
    start(first, 15, 16)
    start(weights, 0, 1, 2, 3)
    loads[3].wait()
    start(gifts, 0)
    spread_rows(x, 1, 1, 8)
    spread_rows(x, 2, 1, 8)
    edge_rows(x, first, 0)
    edge_rows(x, first, 1)
    loads[2].wait()
    acc1[1] = taps(x, w1, 1, 0) + taps(x, w1, 1, 1)
    fast_halo(x, first)
    acc1[1] += taps(x, w1, 1, 2)
    finish_one(1)
    second = halo(y, s2, r2)
    start(second, 12, 10, 11, 13, 14)
    acc1[0] = taps(x, w1, 0, 1) + taps(x, w1, 0, 2)
    arrived(weights, 0, 1)
    start(weights, 4, 5)
    slow_rows(x, first)
    slow_middle(acc1, x, w1)
    finish_one(0, 1, 6)
    start(second, 1, 2, 3, 4, 5, 6)
    slow_corners(x, first)
    slow_edges(acc1, x, w1)
    finish_one(0, 0, 1)
    finish_one(0, 7, 1)
    start(second, 15, 16, 0, 7, 8, 9)

    loads[5].wait()
    edge_rows(y, second, 1)
    acc2[1] = taps(y, w2, 1, 1)
    acc2[0] = taps(y, w2, 0, 2)
    fast_halo(y, second)
    acc2[1] += taps(y, w2, 1, 2)
    edge_rows(y, second, 0)
    acc2[1] += taps(y, w2, 1, 0)
    acc2[0] += taps(y, w2, 0, 1)
    loads[4].wait()
    arrived(weights, 2, 3)
    start(passed, 0, 1)
    slow_rows(y, second)
    slow_middle(acc2, y, w2)
    slow_corners(y, second)
    slow_edges(acc2, y, w2)
    def pool(r, _):
        total = jnp.zeros((64, 256), F32)
        for u in range(2):
            for s in range(2):
                rows = pl.ds(pl.multiple_of(r * 128 + s * 64, 64), 64)
                v = jnp.maximum(acc2[u, rows], 0.0).astype(BF16)
                skip[u + q * (1 - 2 * u), 2 * r + s] = v
                total = total + v.astype(F32)
        halves = []
        for h in range(2):
            tmp[r, h] = total[:, h * 128 : h * 128 + 128]
            even = tmp[r, h, pl.ds(0, 32, stride=2)]
            odd = tmp[r, h, pl.ds(1, 32, stride=2)]
            halves.append(((even + odd) * 0.125).astype(BF16))
        xc[1, row_of, 1 + r] = jnp.concatenate(halves, axis=1)
        return 0
    lax.fori_loop(0, 4, pool, 0, unroll=2)

    partner = across
    shares = [
        pltpu.make_async_remote_copy(
            xc.at[1, row_of, pl.ds(row, n)], xc.at[1, slot, pl.ds(to, n)],
            sg.at[i], rg.at[i], device_id=(b, who), device_id_type=MESH,
        )
        for i, (row, n, slot, to, who) in enumerate(
            [
                (1, 4, row_of, 1, partner),
                (4, 1, chan(1) // nx, 0, chan(1)),
                (4, 1, chan(1) // nx, 0, chan(1 + nx)),
                (1, 1, chan(nc - 1) // nx, 5, chan(nc - 1)),
                (1, 1, chan(nc - 1) // nx, 5, chan(nx - 1)),
            ]
        )
    ]
    for share in shares:
        share.start()
    arrived(gifts, 0)
    start(gifts, *range(1, 2 * nx - 1))
    arrived(weights, 4, 5)
    start(passed, 2)
    for share in shares:
        share.wait_recv()

    def widen(h, r, v):
        xc[0, h, r] = jnp.concatenate([zero_row, v[:-1]], axis=0)
        xc[2, h, r] = jnp.concatenate([v[1:], zero_row], axis=0)

    for h in range(2):
        block = h * nx + place
        for r, valid in ((0, block > 0), (5, block < nc - 1)):
            v = jnp.where(valid, xc[1, h, r].astype(F32), 0.0).astype(BF16)
            xc[1, h, r] = v
            widen(h, r, v)

        def coarse_row(r, _):
            widen(h, r, xc[1, h, r])
            return 0
        lax.fori_loop(1, 5, coarse_row, 0, unroll=4)
    arrived(passed, 0, 1, 2)

    parts = []
    for role, tap, brick in ((0, 2 - 2 * q, slow), (2, 2 * q, fast), (1, 1, b)):
        lhs = jnp.concatenate(
            [xc[k, :, j : j + 4].reshape(256, 256) for j in range(3) for k in range(3)], axis=1
        )
        rhs = jnp.concatenate([wc[tap * 9 + jk] for jk in range(9)], axis=1)
        got = lax.dot_general(lhs, rhs, (((1,), (1,)), ((), ())), preferred_element_type=F32)
        con[role] = got.astype(BF16).reshape(2, 128, 256)
        if role == 1:
            parts[3].wait_recv()
            joint = con[1, 1 - row_of].astype(F32) + rec[2, 1 - row_of].astype(F32)
            con[1, 1 - row_of] = joint.astype(BF16)
        for t, slot, who in ((0, row_of, c), (1, 1 - row_of, partner)):
            if role == 1 and t == 0:
                rec[1, row_of] = con[1, row_of]
                continue
            copy = pltpu.make_async_remote_copy(
                con.at[role, slot],
                rec.at[role, slot if role == 2 else row_of],
                sc.at[role, t], rc.at[role, t],
                device_id=(brick, c if role == 2 else who), device_id_type=MESH,
            )
            copy.start()
            parts.append(copy)
    arrived(gifts, *range(1, 2 * nx - 1))
    for part in parts[:3] + parts[4:]:
        part.wait_recv()

    own = rec[1, row_of].astype(F32) + rec[2, row_of].astype(F32)
    own = own + jnp.where(has_slow, rec[0, row_of].astype(F32), 0.0)
    other = rec[1, 1 - row_of].astype(F32)
    other = other + jnp.where(has_slow, rec[0, 1 - row_of].astype(F32), 0.0)
    own, other = jnp.maximum(own, 0.0), jnp.maximum(other, 0.0)
    cols = [
        jnp.where(row_of == 0, own, other).astype(BF16),
        jnp.where(row_of == 0, other, own).astype(BF16),
    ]
    lifted = jnp.dot(
        jnp.concatenate(cols, axis=1), prj[...].reshape(nc * 64, 256), preferred_element_type=F32
    )
    lift[...] = lifted.reshape(4, 32, 256)

    for copy in first + second + gifts + shares + parts + weights + passed:
        copy.wait_send()


def merge(skip, lift, out, cells, done, rows, tmp, come, go):
    whole = pltpu.make_async_copy(lift, rows, come.at[8])
    whole.start()
    loads = [
        pltpu.make_async_copy(skip.at[u, pl.ds(2 * r, 2)], cells.at[u, r], come.at[2 * r + u])
        for r in range(4) for u in range(2)
    ]
    for load in loads:
        load.start()
    whole.wait()
    stores = []
    for r in range(4):
        for h in range(2):
            piece = rows[r, :, h * 128 : h * 128 + 128]
            tmp[r, h, pl.ds(0, 32, stride=2)] = piece
            tmp[r, h, pl.ds(1, 32, stride=2)] = piece
        wide = jnp.concatenate([tmp[r, 0], tmp[r, 1]], axis=1)
        for u in range(2):
            loads[2 * r + u].wait()
            for s in range(2):
                done[u, r, s] = (cells[u, r, s].astype(F32) + wide).astype(BF16)
            store = pltpu.make_async_copy(done.at[u, r], out.at[u, pl.ds(2 * r, 2)], go.at[2 * r + u])
            store.start()
            stores.append(store)
    for store in stores:
        store.wait()


def shards(nb, nc, volume, first_weight, second_weight, coarse_weight, projection):
    dma = pltpu.SemaphoreType.DMA
    skip, lift = pl.pallas_call(
        functools.partial(level, nb, nc),
        out_shape=(
            jax.ShapeDtypeStruct(volume.shape, BF16),
            jax.ShapeDtypeStruct((4, 32, 256), F32),
        ),
        in_specs=[pl.BlockSpec(memory_space=pl.ANY)] * 5,
        out_specs=(pl.BlockSpec(memory_space=pltpu.VMEM),) * 2,
        scratch_shapes=[
            pltpu.VMEM((3, 4, 10, 64, 256), BF16),
            pltpu.VMEM((3, 4, 10, 64, 256), BF16),
            pltpu.VMEM((3, 2304, 256), BF16),
            pltpu.VMEM((3, 2304, 256), BF16),
            pltpu.VMEM((27, 256, 256), BF16),
            pltpu.VMEM((3, 2, 6, 32, 256), BF16),
            pltpu.VMEM((3, 2, 128, 256), BF16),
            pltpu.VMEM((3, 2, 128, 256), BF16),
            pltpu.VMEM((nc, 64, 256), BF16),
            pltpu.VMEM((2, 512, 256), F32),
            pltpu.VMEM((2, 512, 256), F32),
            pltpu.VMEM((4, 2, 64, 128), F32),
            dma((6,)),
            dma((17,)),
            dma((17,)),
            dma((17,)),
            dma((17,)),
            dma((nc,)),
            dma((nc,)),
            dma((6,)),
            dma((6,)),
            dma((3,)),
            dma((3,)),
            dma((5,)),
            dma((5,)),
            dma((3, 2)),
            dma((3, 2)),
            pltpu.SemaphoreType.REGULAR,
        ],
        compiler_params=pltpu.CompilerParams(
            collective_id=0, has_side_effects=True, vmem_limit_bytes=50 << 20
        ),
        name="level",
    )(
        *(
            pltpu.with_memory_space_constraint(v, pltpu.HBM)
            for v in (
                volume,
                first_weight.reshape(3, 2304, 256),
                second_weight.reshape(3, 2304, 256),
                jnp.swapaxes(coarse_weight, 3, 4).reshape(27, 64, 256),
                projection,
            )
        )
    )
    return pl.pallas_call(
        merge,
        out_shape=jax.ShapeDtypeStruct(volume.shape, BF16),
        in_specs=[pl.BlockSpec(memory_space=pl.ANY)] * 2,
        out_specs=pl.BlockSpec(memory_space=pl.ANY),
        scratch_shapes=[
            pltpu.VMEM((2, 4, 2, 64, 256), BF16),
            pltpu.VMEM((2, 4, 2, 64, 256), BF16),
            pltpu.VMEM((4, 32, 256), F32),
            pltpu.VMEM((4, 2, 64, 128), F32),
            dma((9,)),
            dma((8,)),
        ],
        compiler_params=pltpu.CompilerParams(vmem_limit_bytes=8 << 20),
        name="merge",
    )(skip, lift)


def solution(mesh):
    in_specs = (
        P("brick", "chan", None, None),
        P(),
        P(),
        P(None, None, None, None, "chan"),
        P("chan", None),
    )
    out_specs = P("brick", "chan", None, None)
    body = functools.partial(shards, mesh.shape["brick"], mesh.shape["chan"])
    return jax.shard_map(body, mesh=mesh, in_specs=in_specs, out_specs=out_specs, check_vma=False)
```
